32 devices in a mesh: groups: 2 (over x), feat: 8 (over z, y), tgt: 2 (over core).
Axes of the slice: x: 2, y: 2, z: 4, core: 2. Of those that a mesh axis runs over, the one named last changes fastest.
Arguments:
- inputs: float32 [1536, 2304], P(('groups', 'feat')), parts along dimension 0, may hold values from -6 to 6
- preacts: bfloat16 [1536, 16384], P('groups', 'feat'), parts along dimension 0, may hold values from -6 to 6
- cotangent: float32 [2, 1536, 2304], P('tgt', ('groups', 'feat')), parts along dimension 1, may hold values from -1.5 to 1.5
- w_enc: bfloat16 [2304, 16384], P(None, 'feat'), may hold values from -0.125 to 0.125
- w_dec: bfloat16 [2, 16384, 2304], P('tgt', 'feat'), may hold values from -0.046875 to 0.046875
Outputs:
- grad_dec: float32 [4, 16384, 2304], P(('groups', 'tgt'), 'feat'), parts along dimension 0
- grad_enc: float32 [4608, 16384], P(('groups', 'tgt'), 'feat'), parts along dimension 0
- grad_bias: float32 [32768], P(('groups', 'feat')), parts along dimension 0
- grad_inputs: float32 [1536, 2304], P(('groups', 'feat'), 'tgt'), parts along dimension 0
The draws below stay inside these ranges and needn't reach their ends.
There are 2 independent parts, one for each index of `groups`. The reference program is written for one: setup_inputs(seed, part) draws one part's arguments, and reference() takes and returns one part's arrays. A program takes and returns all parts, laid end to end along the dimension named above; an argument that names none is the same for every part. Nothing has to cross between parts.
All inputs are finite; a program needn't handle non-finite values.
Results may differ from the reference program's by a relative error of at most 0.005.
Values may be sent and summed in bfloat16 or wider, within the bound.
No kernel may reach another device: no remote copies, remote signals or barrier semaphores. Data moves between devices by JAX's collectives and lax.ppermute only.
A program may use at most 128 MiB of HBM per device.

```python
import jax
import jax.numpy as jnp

D = 2304
F = 16384
TOK = 768
LAYERS = 2


def level_of(own_key, shape, pieces, smallest, top_value):
    def one(position, parts):
        steps = jax.random.uniform(jax.random.fold_in(jax.random.fold_in(own_key, 6), position), (parts,), jnp.float32, smallest / len(pieces), top_value / len(pieces))
        return jnp.repeat(jnp.exp(steps), shape[position] // parts).reshape((-1,) + (1,) * (len(shape) - position - 1))

    factor_of = one(*pieces[0])
    for cut in pieces[1:]:
        factor_of = factor_of * one(*cut)
    return factor_of


def noise(key, extent, deviation, bound, shards=(), held_as=jnp.bfloat16):
    level = level_of(key, extent, shards, -0.22, 0.18) if shards else 1.0
    drawn = jax.random.normal(key, extent, jnp.float32) * deviation * level
    return jnp.minimum(jnp.maximum(drawn, -bound), bound).astype(held_as)


def setup_inputs(seed: int = 0, part: int = 0) -> dict:
    streams_of = jax.random.split(jax.random.key(seed), 6)
    own_keys = jax.random.split(jax.random.fold_in(streams_of[5], part), 6)
    return {
        "inputs": noise(own_keys[0], (TOK, D), 1.0, 6.0, ((0, 8),), jnp.float32),
        "preacts": noise(own_keys[1], (TOK, F), 1.0, 6.0, ((1, 8),)),
        "cotangent": noise(own_keys[2], (LAYERS, TOK, D), 0.25, 1.5, ((0, 2), (1, 8)), jnp.float32),
        "w_enc": noise(streams_of[3], (D, F), D ** -0.5, 0.125, ((1, 8),)),
        "w_dec": noise(streams_of[4], (LAYERS, F, D), F ** -0.5, 0.046875, ((0, 2), (1, 8))),
    }


def reference(inputs, preacts, cotangent, w_enc, w_dec):
    active = jnp.maximum(preacts, 0).astype(jnp.bfloat16)
    back_rows = cotangent.astype(jnp.bfloat16)
    grads = []
    feat_grad = jnp.zeros((TOK, F), jnp.float32)
    for layer_idx in range(LAYERS):
        grads.append(jnp.dot(active.T, back_rows[layer_idx], preferred_element_type=jnp.float32))
        feat_grad = feat_grad + jnp.dot(back_rows[layer_idx], w_dec[layer_idx].T, preferred_element_type=jnp.float32)
    grad_dec = jnp.stack(grads)
    pre_grad = jnp.where(preacts > 0, feat_grad, jnp.zeros_like(feat_grad)).astype(jnp.bfloat16)
    input_rows = inputs.astype(jnp.bfloat16)
    grad_enc = jnp.dot(input_rows.T, pre_grad, preferred_element_type=jnp.float32)
    grad_bias = jnp.sum(pre_grad.astype(jnp.float32), axis=0)
    grad_inputs = jnp.dot(pre_grad, w_enc.T, preferred_element_type=jnp.float32)
    return (grad_dec, grad_enc, grad_bias, grad_inputs)
```

```python
import jax
import jax.numpy as jnp
from jax import lax
from jax.sharding import PartitionSpec as P

BF16 = jnp.bfloat16
F32 = jnp.float32


def ring_order(n):
    if n == 8:
        return [0, 2, 4, 6, 7, 5, 3, 1]
    return list(range(n))


def body(inputs, preacts, cotangent, w_enc, w_dec):
    n = lax.axis_size("feat")
    half = n // 2
    order = ring_order(n)
    where_is = [order.index(j) for j in range(n)]
    me = lax.axis_index("feat")
    ring = jnp.array(where_is, jnp.int32)[me]
    order_arr = jnp.array(order, jnp.int32)
    right = [(order[j], order[(j + 1) % n]) for j in range(n)]
    left = [(b, a) for a, b in right]
    ntgt = lax.axis_size("tgt")
    swap = [(j, (j + 1) % ntgt) for j in range(ntgt)]
    tgt_index = lax.axis_index("tgt")
    rows = inputs.shape[0]
    cut = rows // 2
    half_width = inputs.shape[1] // ntgt

    def shard_at(offset):
        return order_arr[jnp.mod(ring + offset, n)]

    def walk(x):
        got = {0: x}
        a = b = x
        for k in range(1, half):
            a = lax.ppermute(a, "feat", right)
            b = lax.ppermute(b, "feat", left)
            got[-k], got[k] = a, b
        a = lax.ppermute(a[:cut], "feat", right)
        b = lax.ppermute(b[cut:], "feat", left)
        got[half] = jnp.concatenate([a, b], 0)
        return got

    back = walk(cotangent[0].astype(BF16))
    input_half = lax.dynamic_slice_in_dim(inputs, tgt_index * half_width, half_width, 1).astype(BF16)
    enc_half = lax.dynamic_slice_in_dim(w_enc, tgt_index * half_width, half_width, 0)

    batches = [[0] + [s * k for k in range(1, half - 1) for s in (-1, 1)], [1 - half, half - 1, half]]
    pre, grads = [], {}
    for batch in batches:
        x = jnp.concatenate([back[o] for o in batch], 0)
        act = jnp.concatenate(
            [lax.dynamic_slice_in_dim(preacts, shard_at(o) * rows, rows, 0) for o in batch], 0
        )
        part = lax.dot_general(
            x, w_dec[0], (((1,), (1,)), ((), ())), preferred_element_type=F32
        ).astype(BF16)
        other = lax.ppermute(part, "tgt", swap)
        summed = part.astype(F32) + other.astype(F32)
        p = jnp.where(act > 0, summed, jnp.zeros_like(summed)).astype(BF16)
        g = lax.dot_general(p, enc_half, (((1,), (1,)), ((), ())), preferred_element_type=F32)
        for j, o in enumerate(batch):
            grads[o] = g[j * rows : (j + 1) * rows]
        pre.append((p, x, act))

    ins = walk(input_half)
    seq = [o for batch in batches for o in batch]
    pre_all = jnp.concatenate([p for p, _, _ in pre], 0)
    back_all = jnp.concatenate([x for _, x, _ in pre], 0)
    act_all = jnp.maximum(jnp.concatenate([a for _, _, a in pre], 0), 0)
    grad_bias = jnp.sum(pre_all.astype(F32), axis=0)
    grad_dec = lax.dot_general(
        act_all, back_all, (((0,), (0,)), ((), ())), preferred_element_type=F32
    )[None]
    input_all = jnp.concatenate([ins[o] for o in seq], 0)
    grad_enc = lax.dot_general(
        input_all, pre_all, (((0,), (0,)), ((), ())), preferred_element_type=F32
    )

    far = grads[half].astype(BF16)
    a = lax.ppermute(far[:cut], "feat", right).astype(F32)
    b = lax.ppermute(far[cut:], "feat", left).astype(F32)
    ga, gb = grads[half - 1], grads[1 - half]
    a = jnp.concatenate([ga[:cut] + a, ga[cut:]], 0)
    b = jnp.concatenate([gb[:cut], gb[cut:] + b], 0)
    for k in range(half - 1, 0, -1):
        a = lax.ppermute(a.astype(BF16), "feat", right).astype(F32) + (grads[k - 1] if k > 1 else 0)
        b = lax.ppermute(b.astype(BF16), "feat", left).astype(F32) + (grads[1 - k] if k > 1 else 0)
    grad_inputs = grads[0] + a + b
    return (grad_dec, grad_enc, grad_bias, grad_inputs)


def solution(mesh):
    in_specs = (
        P(("groups", "feat"), None),
        P("groups", "feat"),
        P("tgt", ("groups", "feat"), None),
        P(None, "feat"),
        P("tgt", "feat", None),
    )
    out_specs = (
        P(("groups", "tgt"), "feat", None),
        P(("groups", "tgt"), "feat"),
        P(("groups", "feat")),
        P(("groups", "feat"), "tgt"),
    )
    return jax.shard_map(body, mesh=mesh, in_specs=in_specs, out_specs=out_specs, check_vma=False)
```
